512 devices in a mesh: grp: 16 (over z_lo, core), seq: 32 (over x, z_hi, y).
Axes of the slice: x: 4, y: 4, z: 16 (z_hi: 2, z_lo: 8; z = z_hi * 8 + z_lo), core: 2. Of those that a mesh axis runs over, the one named last changes fastest.
Arguments:
- queries: bfloat16 [65536, 3072], P(('grp', 'seq')), may hold values from -6 to 6, as said below
- key_states: bfloat16 [65536, 3072], P(('grp', 'seq')), may hold values from -6 to 6
- value_states: bfloat16 [65536, 3072], P(('grp', 'seq')), may hold values from -16 to 16
- key_keep: int32 [65536], P(('grp', 'seq')), may hold values 0 or 1
- summary_pos: int32 [16], replicated, may hold values from 0 to 31
Outputs:
- attended: bfloat16 [65536, 3072], P(('grp', 'seq'))
The draws below stay inside these ranges and needn't reach their ends.
Inputs may be any that keep to these rules, and one draw needn't show every extreme that they name: queries and key_states entries lie within -6 to 6.
All inputs are finite; a program needn't handle non-finite values. No bound on the sum of `key_keep` on one device may be relied on, other than what follows from the above.
Results may differ from the reference program's by a relative error of at most 0.008.
Values may be sent and summed in bfloat16 or wider, within the bound.
No kernel may reach another device: no remote copies, remote signals or barrier semaphores. Data moves between devices by JAX's collectives and lax.ppermute only.
A program may use at most 64 MiB of HBM per device.

```python
import math
import jax
import jax.numpy as jnp
from jax import lax

HEADS = 24
HEAD_DIM = 128
FIXED_HEADS = 4
LOCAL_HEADS = 16
BLOCK = 128
LOOKBACK = 2
STRIDE = 32
WINDOWS = 16
BLOCKS = 512
TOKENS = 65536


def draw_pair(key):
    full_shape = (TOKENS, HEADS * HEAD_DIM)
    query_base = jnp.clip(jax.random.normal(jax.random.fold_in(key, 1), full_shape, jnp.float32), -6.0, 6.0)
    key_base = jnp.clip(1.5 * jax.random.normal(jax.random.fold_in(key, 2), full_shape, jnp.float32), -6.0, 6.0)
    return (query_base, key_base)


def draw_queries(key, part):
    return draw_pair(key)[0].astype(jnp.bfloat16)


def draw_key_states(key, part):
    return draw_pair(key)[1].astype(jnp.bfloat16)


def place_ends(result, stream_key, smallest, high):
    longest = result.shape.index(max(result.shape))
    spots = []
    for shift in (0, 1):
        where = [jax.random.randint(jax.random.fold_in(stream_key, axis), (), 0, length) for axis, length in enumerate(result.shape)]
        where[longest] = (where[longest] + shift) % result.shape[longest]
        spots.append(tuple(where))
    return result.at[spots[0]].set(smallest).at[spots[1]].set(high)


def block_scale(rng, dims, cuts, low, largest):
    def one(dim, blocks):
        steps = jax.random.uniform(jax.random.fold_in(jax.random.fold_in(rng, 6), dim), (blocks,), jnp.float32, low / len(cuts), largest / len(cuts))
        return jnp.repeat(jnp.exp(steps), dims[dim] // blocks).reshape((-1,) + (1,) * (len(dims) - dim - 1))

    loudness = one(*cuts[0])
    for cut in cuts[1:]:
        loudness = loudness * one(*cut)
    return loudness


def centred(stream_key, shape, scale, most, pieces=(), held_as=jnp.bfloat16):
    level = block_scale(stream_key, shape, pieces, -0.22, 0.18) if pieces else 1.0
    values = jax.random.normal(stream_key, shape, jnp.float32) * scale * level
    return jnp.minimum(jnp.maximum(values, -most), most).astype(held_as)


def setup_inputs(seed: int = 0) -> dict:
    keys = jax.random.split(jax.random.key(seed), 6)
    return {
        "queries": draw_queries(jax.random.fold_in(keys[5], 71), 0),
        "key_states": draw_key_states(jax.random.fold_in(keys[5], 71), 0),
        "value_states": centred(keys[2], (TOKENS, HEADS * HEAD_DIM), 4.0, 16.0, ((0, 512),)),
        "key_keep": place_ends((jax.random.randint(keys[3], (TOKENS,), 0, 8) < 7).astype(jnp.int32), jax.random.fold_in(keys[3], 1), 0, 1),
        "summary_pos": place_ends(jax.random.randint(keys[4], (WINDOWS,), 0, STRIDE), jax.random.fold_in(keys[4], 1), 0, STRIDE - 1).astype(jnp.int32),
    }


NEG = -1e+30

def softmax_attend(query_heads, key_heads, value_heads, allowed):
    scores = jnp.einsum('hqd,hkd->hqk', query_heads, key_heads) / math.sqrt(HEAD_DIM)
    scores = jnp.where(allowed[None], scores, NEG)
    row_max = lax.optimization_barrier(jnp.max(scores, axis=2, keepdims=True))
    weights = jnp.where(allowed[None], jnp.exp(scores - row_max), 0.0)
    row_sum = lax.optimization_barrier(jnp.sum(weights, axis=2, keepdims=True))
    rounded = lax.optimization_barrier(weights.astype(jnp.bfloat16)).astype(jnp.float32)
    weighted = jnp.einsum('hqk,hkd->hqd', rounded, value_heads)
    return weighted / row_sum

def heads_first(block_rows):
    return jnp.transpose(block_rows.astype(jnp.float32), (1, 0, 2))

def reference(queries, key_states, value_states, key_keep, summary_pos):
    query_blocks = queries.reshape(BLOCKS, BLOCK, HEADS, HEAD_DIM)
    key_blocks = key_states.reshape(BLOCKS, BLOCK, HEADS, HEAD_DIM)
    value_blocks = value_states.reshape(BLOCKS, BLOCK, HEADS, HEAD_DIM)
    keep_blocks = key_keep.reshape(BLOCKS, BLOCK)
    windows = jnp.arange(WINDOWS, dtype=jnp.int32)
    lane_ids = jnp.arange(BLOCK, dtype=jnp.int32)
    fixed_lo = LOCAL_HEADS
    fixed_hi = LOCAL_HEADS + FIXED_HEADS

    def one_block(block_id):
        window = block_id // STRIDE
        column = block_id % STRIDE
        query_pos = block_id * BLOCK + lane_ids
        near_ids = block_id - LOOKBACK + jnp.arange(LOOKBACK + 1, dtype=jnp.int32)
        near_valid = near_ids >= 0
        near_safe = jnp.maximum(near_ids, 0).astype(jnp.int32)
        key_pos = (near_safe[:, None] * BLOCK + lane_ids[None, :]).reshape(-1)
        near_keep = keep_blocks[near_safe].reshape(-1) == 1
        valid_rep = jnp.repeat(near_valid, BLOCK)
        diagonal = key_pos[None, :] == query_pos[:, None]
        near_allowed = valid_rep[None, :] & (key_pos[None, :] <= query_pos[:, None]) & (near_keep[None, :] | diagonal)
        query_heads = heads_first(query_blocks[block_id])
        key_heads = heads_first(key_blocks[near_safe].reshape(-1, HEADS, HEAD_DIM))
        value_heads = heads_first(value_blocks[near_safe].reshape(-1, HEADS, HEAD_DIM))

        def far_part(blocks, valid, head_lo, head_hi):
            far_keys = key_blocks[blocks][:, :, head_lo:head_hi].reshape(-1, head_hi - head_lo, HEAD_DIM)
            far_values = value_blocks[blocks][:, :, head_lo:head_hi].reshape(-1, head_hi - head_lo, HEAD_DIM)
            far_keep = keep_blocks[blocks].reshape(-1) == 1
            far_valid = jnp.repeat(valid, BLOCK) & far_keep
            allowed = jnp.concatenate([near_allowed, jnp.broadcast_to(far_valid[None, :], (BLOCK, far_valid.shape[0]))], axis=1)
            all_keys = jnp.concatenate([key_heads[head_lo:head_hi], heads_first(far_keys)], axis=1)
            all_values = jnp.concatenate([value_heads[head_lo:head_hi], heads_first(far_values)], axis=1)
            return softmax_attend(query_heads[head_lo:head_hi], all_keys, all_values, allowed)
        fixed_blocks = (windows * STRIDE + summary_pos).astype(jnp.int32)
        fixed_valid = fixed_blocks < block_id - LOOKBACK
        strided_blocks = (windows * STRIDE + column).astype(jnp.int32)
        strided_valid = windows < window
        local_out = softmax_attend(query_heads[:fixed_lo], key_heads[:fixed_lo], value_heads[:fixed_lo], near_allowed)
        fixed_out = far_part(fixed_blocks, fixed_valid, fixed_lo, fixed_hi)
        strided_out = far_part(strided_blocks, strided_valid, fixed_hi, HEADS)
        weighted = jnp.concatenate([local_out, fixed_out, strided_out], axis=0)
        return jnp.transpose(weighted, (1, 0, 2)).reshape(BLOCK, HEADS * HEAD_DIM).astype(jnp.bfloat16)
    attended = lax.map(one_block, jnp.arange(BLOCKS, dtype=jnp.int32))
    return attended.reshape(TOKENS, HEADS * HEAD_DIM)
```

```python
import math

import jax
import jax.numpy as jnp
from jax import lax
from jax.experimental import pallas as pl
from jax.experimental.pallas import tpu as pltpu
from jax.sharding import Mesh, PartitionSpec as P

HEADS = 24
DIM = 128
BLOCK = 128
LOCAL = 16
ZL, CORES, XS, ZH, YS = 8, 2, 4, 2, 4
AXES = ("zl", "core", "x", "zh", "y")
SIZES = dict(zip(AXES, (ZL, CORES, XS, ZH, YS)))
MINE = HEADS // YS
PER = LOCAL // YS
WIDE = MINE * DIM
FIX, STR = PER, PER + 1
FLAG_ROWS = 16
MARK = 128.0
NEG = -1e30
SCALE = 1.0 / (math.sqrt(DIM) * math.log(2.0))
f32, bf16 = jnp.float32, jnp.bfloat16


def index_of(place):
    at = 0
    for axis in AXES:
        at = at * SIZES[axis] + place[axis]
    return at


def route(move):
    pairs = []
    for zl in range(ZL):
        for core in range(CORES):
            for x in range(XS):
                for zh in range(ZH):
                    for y in range(YS):
                        place = dict(zl=zl, core=core, x=x, zh=zh, y=y)
                        to = move(place)
                        if to is not None:
                            pairs.append((index_of(place), index_of({**place, **to})))
    return pairs


def send(value, move):
    return lax.ppermute(value, AXES, route(move))


def next_group(p):
    if p["zh"] == 0:
        return dict(zh=1)
    if p["x"] < XS - 1:
        return dict(zh=0, x=p["x"] + 1)
    window = p["zl"] * CORES + p["core"] + 1
    if window == ZL * CORES:
        return None
    return dict(zh=0, x=0, zl=window // CORES, core=window % CORES)


def up(distance):
    return lambda p: dict(zl=p["zl"] + distance) if p["zl"] + distance < ZL else None


def other_core(p):
    return dict(core=1 - p["core"])


def head_parts(rows):
    fixed, strided = LOCAL * DIM, (LOCAL + YS) * DIM
    return jnp.stack(
        [
            jnp.concatenate(
                [
                    rows[:, y * PER * DIM : (y + 1) * PER * DIM],
                    rows[:, fixed + y * DIM : fixed + (y + 1) * DIM],
                    rows[:, strided + y * DIM : strided + (y + 1) * DIM],
                ],
                axis=1,
            )
            for y in range(YS)
        ]
    )


def qk(a, b):
    return lax.dot_general(a, b, (((1,), (1,)), ((), ())), preferred_element_type=f32)


def pv(p, v):
    return jnp.dot(p.astype(bf16), v, preferred_element_type=f32)


def attend(info, far_ok, q, kv, halo, fx, s1, s2, e1, e2, out, m_sc, l_sc, a_sc):
    has_prev = info[0]
    core = info[1]
    rows = lax.broadcasted_iota(jnp.int32, (BLOCK, BLOCK), 0)
    cols = lax.broadcasted_iota(jnp.int32, (BLOCK, BLOCK), 1)
    pick = jnp.where(lax.broadcasted_iota(jnp.int32, (16, DIM), 1) == 0, 1.0, 0.0).astype(bf16)

    def own_mask(j):
        keep = kv[j, 2 * BLOCK : 2 * BLOCK + 1, 0:BLOCK].astype(f32) > 0.5
        return keep

    keeps = [own_mask(j) for j in range(YS)]
    halo_keep = []
    for i in range(2):
        flag = qk(pick, halo[i, 0:BLOCK, 0:DIM])[0:1]
        halo_keep.append((flag < MARK / 2) & (has_prev > 0))

    for j in range(YS):
        own_ok = ((cols <= rows) & jnp.broadcast_to(keeps[j], (BLOCK, BLOCK))) | (cols == rows)
        oks = [own_ok]
        for back in (1, 2):
            flag = keeps[j - back] if j >= back else halo_keep[2 + j - back]
            oks.append(jnp.broadcast_to(flag, (BLOCK, BLOCK)))
        for h in range(MINE):
            lo, hi = h * DIM, (h + 1) * DIM
            query = q[j, :, lo:hi]
            scores, values = [], []
            for back in range(3):
                if j >= back:
                    key = kv[j - back, 0:BLOCK, lo:hi]
                    value = kv[j - back, BLOCK : 2 * BLOCK, lo:hi]
                else:
                    key = halo[2 + j - back, 0:BLOCK, lo:hi]
                    value = halo[2 + j - back, BLOCK : 2 * BLOCK, lo:hi]
                scores.append(jnp.where(oks[back], qk(query, key) * SCALE, NEG))
                values.append(value)
            top = jnp.maximum(jnp.maximum(scores[0], scores[1]), scores[2])
            top = jnp.max(top, axis=1, keepdims=True)
            weights = [jnp.exp2(s - top) for s in scores]
            total = jnp.sum(weights[0] + weights[1] + weights[2], axis=1, keepdims=True)
            acc = pv(weights[0], values[0]) + pv(weights[1], values[1]) + pv(weights[2], values[2])
            if h < PER:
                out[j, :, lo:hi] = (acc / total).astype(bf16)
            else:
                m_sc[h - PER, j] = top
                l_sc[h - PER, j] = total
                a_sc[h - PER, j] = acc

    def far(kind, j, parts):
        lo, hi = (PER + kind) * DIM, (PER + kind + 1) * DIM
        query = q[j, :, lo:hi]
        top = m_sc[kind, j]
        scores = []
        for rows_, ok in parts:
            key = rows_[:, 0:DIM]
            flag = qk(pick, key)[0:1]
            allowed = (flag < MARK / 2) & (ok > 0.5)
            s = jnp.where(jnp.broadcast_to(allowed, (BLOCK, key.shape[0])), qk(query, key) * SCALE, NEG)
            scores.append(s)
            top = jnp.maximum(top, jnp.max(s, axis=1, keepdims=True))
        shrink = jnp.exp2(m_sc[kind, j] - top)
        total = l_sc[kind, j] * shrink
        acc = a_sc[kind, j] * shrink
        for s, (rows_, ok) in zip(scores, parts):
            w = jnp.exp2(s - top)
            total = total + jnp.sum(w, axis=1, keepdims=True)
            acc = acc + pv(w, rows_[:, DIM : 2 * DIM])
        out[j, :, lo:hi] = (acc / total).astype(bf16)

    for j in range(YS):
        far(0, j, [(fx[...], far_ok[j : j + 1, :])])
    per = 2 * 4 * BLOCK
    for side, (near_items, far_items) in enumerate(((s1, s2), (e1, e2))):
        column_pair = core if side == 0 else 1 - core
        for jj in range(2):
            j = 2 * column_pair + jj
            parts = []
            for t, items in enumerate((near_items, far_items)):
                rows_ = items[:, :, jj].reshape(per, 2 * DIM)
                parts.append((rows_, far_ok[4 : 5, t * per : (t + 1) * per]))
            far(1, j, parts)


def on_device(queries, key_states, value_states, key_keep, summary_pos):
    zl, core, x, zh, y = (lax.axis_index(a) for a in AXES)
    window = zl * CORES + core
    group = window * (XS * ZH) + x * ZH + zh

    flags = jnp.broadcast_to(key_keep.astype(bf16)[None, None, :], (YS, FLAG_ROWS, BLOCK))
    flags = jnp.pad(flags, ((0, 0), (0, 0), (0, WIDE - BLOCK)))
    packed = jnp.concatenate([head_parts(key_states), head_parts(value_states), flags], axis=1)
    kv = lax.all_to_all(packed, "y", 0, 0)
    q = lax.all_to_all(head_parts(queries), "y", 0, 0)

    keep = kv[:, 2 * BLOCK, :BLOCK] > 0.5
    keys = jnp.where(keep[:, :, None], kv[:, :BLOCK], MARK).astype(bf16)
    vals = kv[:, BLOCK : 2 * BLOCK]
    halo = send(jnp.concatenate([keys[2:], vals[2:]], axis=1), next_group)

    cut = slice(STR * DIM, (STR + 1) * DIM)
    strided = jnp.concatenate([keys[:, :, cut], vals[:, :, cut]], axis=2)
    stay = jnp.where(core == 0, strided[:2], strided[2:])
    leave = jnp.where(core == 0, strided[2:], strided[:2])
    come = send(leave, other_core)
    first = jnp.where(core == 0, jnp.stack([stay, come]), jnp.stack([come, stay]))[None]
    r1 = send(first, up(4))
    two = jnp.concatenate([first, r1])
    r2 = send(two, up(2))
    s1 = jnp.concatenate([two, r2])
    s2 = send(s1, up(1))
    e1 = send(s1, other_core)
    e2 = send(s2, other_core)

    cut = slice(FIX * DIM, (FIX + 1) * DIM)
    fixed = jnp.concatenate([keys[:, :, cut], vals[:, :, cut]], axis=2)
    root = summary_pos[window]
    root_x, root_zh, root_y = root // (ZH * YS), (root // YS) % ZH, root % YS
    block = lax.dynamic_index_in_dim(fixed, root_y, 0, keepdims=False)
    quarters = lax.all_to_all(block.reshape(XS, BLOCK // XS, 2 * DIM), "x", 0, 0)
    piece = lax.dynamic_index_in_dim(quarters, root_x, 0, keepdims=False)
    twin = send(piece, lambda p: dict(zh=1 - p["zh"]))
    piece = jnp.where(zh == root_zh, piece, twin)
    pieces = jnp.broadcast_to(piece[None], (ZL * CORES,) + piece.shape)
    pieces = lax.all_to_all(pieces, ("zl", "core"), 0, 0)
    pieces = jnp.broadcast_to(pieces[None], (XS,) + pieces.shape)
    pieces = lax.all_to_all(pieces, "x", 0, 0)
    fx = pieces.reshape(-1, 2 * DIM)

    windows = jnp.arange(ZL * CORES, dtype=jnp.int32)
    block_ids = group * YS + jnp.arange(YS, dtype=jnp.int32)
    fixed_ok = (windows * (XS * ZH * YS) + summary_pos)[None, :] < block_ids[:, None] - 2
    fixed_ok = jnp.broadcast_to(fixed_ok[:, None, :, None], (YS, XS, ZL * CORES, BLOCK // XS)).reshape(YS, -1)
    chips = zl - jnp.array([0, 4, 2, 6, 1, 5, 3, 7], jnp.int32)
    their = chips[:, None] * CORES + jnp.arange(CORES, dtype=jnp.int32)[None, :]
    strided_ok = (chips[:, None] >= 0) & (their < window)
    strided_ok = jnp.broadcast_to(strided_ok[:, :, None], (ZL, CORES, BLOCK)).reshape(1, -1)
    far_ok = jnp.concatenate([fixed_ok, strided_ok, strided_ok, strided_ok, strided_ok]).astype(f32)
    info = jnp.stack([(group > 0).astype(jnp.int32), core.astype(jnp.int32)])

    vmem = pl.BlockSpec(memory_space=pltpu.VMEM)
    out = pl.pallas_call(
        attend,
        out_shape=jax.ShapeDtypeStruct((YS, BLOCK, WIDE), bf16),
        in_specs=[pl.BlockSpec(memory_space=pltpu.SMEM)] + [vmem] * 9,
        out_specs=vmem,
        scratch_shapes=[
            pltpu.VMEM((2, YS, BLOCK, 1), f32),
            pltpu.VMEM((2, YS, BLOCK, 1), f32),
            pltpu.VMEM((2, YS, BLOCK, DIM), f32),
        ],
        compiler_params=pltpu.CompilerParams(vmem_limit_bytes=48 << 20),
        name="attend",
    )(info, far_ok, q, kv, halo, fx, s1, s2, e1, e2)
    back = lax.all_to_all(out, "y", 0, 0)
    near = [back[i, :, : PER * DIM] for i in range(YS)]
    fixed = [back[i, :, FIX * DIM : STR * DIM] for i in range(YS)]
    strided = [back[i, :, STR * DIM :] for i in range(YS)]
    return jnp.concatenate(near + fixed + strided, axis=1)


def solution(mesh):
    fine = Mesh(mesh.devices.reshape(ZL, CORES, XS, ZH, YS), AXES)
    return jax.shard_map(
        on_device,
        mesh=fine,
        in_specs=(P(AXES, None), P(AXES, None), P(AXES, None), P(AXES), P()),
        out_specs=P(AXES, None),
        check_vma=False,
    )
```

```python
import itertools
import math

import jax
import jax.numpy as jnp
from jax import lax
from jax.experimental import pallas as pl
from jax.experimental.pallas import tpu as pltpu
from jax.sharding import Mesh, PartitionSpec as P

HEADS = 24
DIM = 128
BLOCK = 128
LOCAL = 16
ZP, ZQ, CORES, XS, ZH, YS = 4, 2, 2, 4, 2, 4
AXES = ("zp", "zq", "core", "x", "zh", "y")
SIZES = dict(zip(AXES, (ZP, ZQ, CORES, XS, ZH, YS)))
GRP = ("zp", "zq", "core")
WINDOWS = ZP * ZQ * CORES
PART = BLOCK // YS
PER = LOCAL // YS
MINE = PER + 2
WIDE = MINE * DIM
ROWS = 2 * BLOCK + 16
MARK = 128.0
NEG = -1e30
LEGS = (4, 4)
LEAST = -1e4
SCALE = 1.0 / (math.sqrt(DIM) * math.log(2.0))
f32, bf16 = jnp.float32, jnp.bfloat16


def index_of(place):
    at = 0
    for axis in AXES:
        at = at * SIZES[axis] + place[axis]
    return at


def route(move):
    pairs = []
    for spot in itertools.product(*(range(SIZES[a]) for a in AXES)):
        place = dict(zip(AXES, spot))
        to = move(place)
        if to is not None:
            pairs.append((index_of(place), index_of({**place, **to})))
    return pairs


def send(value, move):
    return lax.ppermute(value, AXES, route(move))


def next_group(p):
    if p["zh"] == 0:
        return dict(p, zh=1)
    if p["x"] < XS - 1:
        return dict(p, zh=0, x=p["x"] + 1)
    window = (p["zp"] * ZQ + p["zq"]) * CORES + p["core"] + 1
    if window == WINDOWS:
        return None
    return dict(p, zh=0, x=0, zp=window // (ZQ * CORES), zq=window // CORES % ZQ, core=window % CORES)


def along_z(p, steps):
    z = (p["zh"] * ZP + p["zp"]) * ZQ + p["zq"]
    z = (z + (steps if p["core"] == 0 else -steps)) % (ZH * ZP * ZQ)
    return dict(p, zh=z // (ZP * ZQ), zp=z // ZQ % ZP, zq=z % ZQ)


def leg(n):
    pairs = []
    for spot in itertools.product(*(range(SIZES[a]) for a in AXES)):
        place = dict(zip(AXES, spot))
        end = next_group(place)
        if end is not None:
            to = along_z(place, sum(LEGS[: n + 1])) if n < len(LEGS) - 1 else end
            pairs.append((index_of(along_z(place, sum(LEGS[:n]))), index_of(to)))
    return pairs


def flip(axis, bits):
    return lambda p: {axis: p[axis] ^ bits}


def heads_of(y):
    return [PER * y + i for i in range(PER)] + [LOCAL + y, LOCAL + YS + y]


def qk(a, b):
    return lax.dot_general(a, b, (((1,), (1,)), ((), ())), preferred_element_type=f32)


def pv(p, v):
    return jnp.dot(p.astype(bf16), v, preferred_element_type=f32)


def unmarked(keys):
    rows = 16
    pick = jnp.where(lax.broadcasted_iota(jnp.int32, (rows, DIM), 1) == 0, 1.0, 0.0).astype(bf16)
    return qk(pick, keys)[0:1] < MARK / 2


def column(head):
    return slice(head * DIM, (head + 1) * DIM)


def pack_kernel(info, keep_row, keep_col, q, k, v, s1, f1, *outs):
    pieces, queries = outs[:YS], outs[YS:]
    keep = jnp.broadcast_to(keep_col[...] > 0, (BLOCK, DIM))
    for h in range(YS):
        c = column(LOCAL + YS + h)
        key = jnp.where(keep, k[:, c], jnp.array(MARK, bf16))
        for s in range(BLOCK // PART):
            r = slice(s * PART, (s + 1) * PART)
            s1[h * YS + s, :, 0:DIM] = key[r]
            s1[h * YS + s, :, DIM : 2 * DIM] = v[r, c]
            s1[h * YS + s, :, 2 * DIM : 3 * DIM] = q[r, c]
        c = column(LOCAL + h)
        key = jnp.where(keep, k[:, c], jnp.array(MARK, bf16))
        for s in range(XS):
            r = slice(s * PART, (s + 1) * PART)
            f1[s * YS + h, :, 0:DIM] = key[r]
            f1[s * YS + h, :, DIM : 2 * DIM] = v[r, c]
    row = jnp.broadcast_to(keep_row[...].astype(f32), (16, BLOCK)).astype(bf16)
    for here in range(YS):

        @pl.when(info[1] == here)
        def _():
            for d in range(YS):
                for i, h in enumerate(heads_of(here ^ d)):
                    to = column(i)
                    pieces[d][0:BLOCK, to] = k[:, column(h)]
                    pieces[d][BLOCK : 2 * BLOCK, to] = v[:, column(h)]
                    pieces[d][2 * BLOCK : ROWS, to] = row
                    queries[d][:, to] = q[:, column(h)]


def halo_kernel(info, *refs):
    out = refs[-1]
    for here in range(YS):

        @pl.when(info[1] == here)
        def _():
            for i in range(2):
                ref = refs[here ^ (2 + i)]
                row = ref[2 * BLOCK : 2 * BLOCK + 1, 0:BLOCK].astype(f32)
                keep = jnp.transpose(jnp.broadcast_to(row, (BLOCK, BLOCK))) > 0.5
                for h in range(MINE):
                    c = column(h)
                    out[i, 0:BLOCK, c] = jnp.where(keep, ref[0:BLOCK, c], jnp.array(MARK, bf16))
                out[i, BLOCK : 2 * BLOCK] = ref[BLOCK : 2 * BLOCK]


def stats_of(top, total, shape):
    rough = total.astype(bf16).astype(f32)
    lanes = lax.broadcasted_iota(jnp.int32, shape, 1)
    return jnp.where(lanes == 0, top, jnp.where(lanes == 1, rough, total - rough)).astype(bf16)


def far_kernel(part, keys_values, out):
    count = WINDOWS * BLOCK
    kv = keys_values[...].reshape(count, 2 * DIM)
    flags = unmarked(kv[:, :DIM])
    step = 128
    for t in range(WINDOWS * PART // step):
        windows = step // PART
        query = part[t * windows : (t + 1) * windows, :, 2 * DIM : 3 * DIM].reshape(step, DIM)
        row_window = t * windows + lax.broadcasted_iota(jnp.int32, (step, count), 0) // PART
        key_window = lax.broadcasted_iota(jnp.int32, (step, count), 1) // PART % WINDOWS
        ok = (key_window < row_window) & jnp.broadcast_to(flags, (step, count))
        scores = jnp.where(ok, qk(query, kv[:, :DIM]) * SCALE, NEG)
        top = jnp.maximum(jnp.max(scores, axis=1, keepdims=True), LEAST)
        top = top.astype(bf16).astype(f32)
        weights = jnp.exp2(scores - top)
        total = jnp.sum(weights, axis=1, keepdims=True)
        acc = pv(weights, kv[:, DIM:])
        both = jnp.concatenate([acc.astype(bf16), stats_of(top, total, (step, DIM))], axis=1)
        out[t * windows : (t + 1) * windows] = both.reshape(windows, PART, 2 * DIM)


def attend_kernel(info, fixed_ok, p0, p1, p2, p3, q0, q1, q2, q3, halo, f0, f1, f2, f3, out, kv, q):
    for d, (piece, query) in enumerate(zip((p0, p1, p2, p3), (q0, q1, q2, q3))):
        kv[info[1] ^ d] = piece[...]
        q[info[1] ^ d] = query[...]
    summary = (f0, f1, f2, f3)
    rows = lax.broadcasted_iota(jnp.int32, (BLOCK, BLOCK), 0)
    cols = lax.broadcasted_iota(jnp.int32, (BLOCK, BLOCK), 1)
    keeps = [kv[j, 2 * BLOCK : 2 * BLOCK + 1, 0:BLOCK].astype(f32) > 0.5 for j in range(YS)]
    halo_keeps = [unmarked(halo[i, 0:BLOCK, 0:DIM]) & (info[0] > 0) for i in range(2)]
    far_flags = [unmarked(f[:, 0:DIM]) for f in summary]
    for j in range(YS):
        masks = [((cols <= rows) & jnp.broadcast_to(keeps[j], (BLOCK, BLOCK))) | (cols == rows)]
        for back in (1, 2):
            flag = keeps[j - back] if j >= back else halo_keeps[2 + j - back]
            masks.append(jnp.broadcast_to(flag, (BLOCK, BLOCK)))
        for h in range(MINE):
            c = column(h)
            query = q[j, :, c]
            scores, values = [], []
            for back in range(3):
                ref, at = (kv, j - back) if j >= back else (halo, 2 + j - back)
                scores.append(jnp.where(masks[back], qk(query, ref[at, 0:BLOCK, c]) * SCALE, NEG))
                values.append(ref[at, BLOCK : 2 * BLOCK, c])
            if h == PER:
                for f, flag in zip(summary, far_flags):
                    ok = flag & (fixed_ok[j : j + 1, :] > 0.5)
                    s = qk(query, f[:, 0:DIM]) * SCALE
                    scores.append(jnp.where(jnp.broadcast_to(ok, s.shape), s, NEG))
                    values.append(f[:, DIM : 2 * DIM])
            top = jnp.max(jnp.maximum(jnp.maximum(scores[0], scores[1]), scores[2]), axis=1, keepdims=True)
            for s in scores[3:]:
                top = jnp.maximum(top, jnp.max(s, axis=1, keepdims=True))
            if h == PER + 1:
                top = top.astype(bf16).astype(f32)
            weights = [jnp.exp2(s - top) for s in scores]
            total = jnp.sum(weights[0] + weights[1] + weights[2], axis=1, keepdims=True)
            acc = pv(weights[0], values[0]) + pv(weights[1], values[1]) + pv(weights[2], values[2])
            for w, v in zip(weights[3:], values[3:]):
                total = total + jnp.sum(w, axis=1, keepdims=True)
                acc = acc + pv(w, v)
            if h == PER + 1:
                out[j, :, c] = acc.astype(bf16)
                out[j, :, column(h + 1)] = stats_of(top, total, (BLOCK, DIM))
            else:
                out[j, :, c] = (acc / total).astype(bf16)


def merge_kernel(back, far, out):
    for y in range(YS):
        for i, h in enumerate(heads_of(y)[:-1]):
            out[:, column(h)] = back[y, :, column(i)]
        near = back[y, :, column(MINE)].astype(f32)
        there = far[y, :, column(1)].astype(f32)
        near_top, near_total = near[:, 0:1], near[:, 1:2] + near[:, 2:3]
        far_top, far_total = there[:, 0:1], there[:, 1:2] + there[:, 2:3]
        top = jnp.maximum(near_top, far_top)
        near_scale, far_scale = jnp.exp2(near_top - top), jnp.exp2(far_top - top)
        acc = back[y, :, column(MINE - 1)].astype(f32) * near_scale
        acc = acc + far[y, :, column(0)].astype(f32) * far_scale
        total = near_total * near_scale + far_total * far_scale
        out[:, column(heads_of(y)[-1])] = (acc / total).astype(bf16)


VMEM = pl.BlockSpec(memory_space=pltpu.VMEM)
SMEM = pl.BlockSpec(memory_space=pltpu.SMEM)


def call(kernel, shapes, flops, operands, scratch=()):
    many = isinstance(shapes, list)
    moved = sum(o.size * o.dtype.itemsize for o in operands)
    outs = [jax.ShapeDtypeStruct(s, bf16) for s in shapes] if many else jax.ShapeDtypeStruct(shapes, bf16)
    return pl.pallas_call(
        kernel,
        out_shape=outs,
        in_specs=[SMEM if o.ndim == 1 else VMEM for o in operands],
        out_specs=[VMEM] * len(shapes) if many else VMEM,
        scratch_shapes=scratch,
        compiler_params=pltpu.CompilerParams(vmem_limit_bytes=40 << 20),
        cost_estimate=pl.CostEstimate(flops=flops, bytes_accessed=moved, transcendentals=0),
        name=kernel.__name__,
    )(*operands)


tie = lax.optimization_barrier
DOUBLING = (("zp", 2, 8), ("zp", 1, 4), ("zq", 1, 2), ("core", 1, 1))


def on_device(queries, key_states, value_states, key_keep, summary_pos):
    zp, zq, core, x, zh, y = (lax.axis_index(a) for a in AXES)
    window = (zp * ZQ + zq) * CORES + core
    group = window * (XS * ZH) + x * ZH + zh
    info = jnp.stack([(group > 0).astype(jnp.int32), y.astype(jnp.int32)])

    windows = jnp.arange(WINDOWS, dtype=jnp.int32)
    masks = [0]
    for _, bit, mask in DOUBLING:
        masks += [m ^ mask for m in masks]
    order = window ^ jnp.array(masks, jnp.int32)
    where = jnp.sum(jnp.where(order[:, None] == windows[None, :], summary_pos[None, :], 0), axis=1)
    block_ids = group * YS + jnp.arange(YS, dtype=jnp.int32)
    fixed_ok = (order * (XS * ZH * YS) + where)[None, :] < block_ids[:, None] - 2
    fixed_ok = jnp.repeat(fixed_ok.astype(f32), PART, axis=1)

    shapes = [(WINDOWS, PART, 3 * DIM), (XS * YS, PART, 2 * DIM)] + [(ROWS, WIDE)] * YS + [(BLOCK, WIDE)] * YS
    keep_row, keep_col = key_keep.reshape(1, BLOCK), key_keep.reshape(BLOCK, 1)
    packed = call(pack_kernel, shapes, 10**6, [info, keep_row, keep_col, queries, key_states, value_states])
    s1, f1, pieces, asked = packed[0], packed[1], packed[2 : 2 + YS], packed[2 + YS :]

    root = summary_pos[window]
    at = root // (ZH * YS) * YS + root % YS
    here = zh == root // YS % ZH
    got = [pieces[0]] + [send(pieces[d], flip("y", d)) for d in range(1, YS)]
    parts = lax.all_to_all(f1, ("x", "y"), 0, 0)
    parts, s1 = tie((parts, s1))
    part = lax.all_to_all(s1, GRP, 0, 0)
    piece = lax.dynamic_index_in_dim(parts, at, 0, keepdims=False)
    twin = send(piece, flip("zh", 1))
    spread = jnp.where(here, piece, twin)
    got1, got2, got3, part, spread, asked = tie((got[1], got[2], got[3], part, spread, asked))
    got = [got[0], got1, got2, got3]
    halo = call(halo_kernel, (2, 2 * BLOCK, WIDE), 10**6, [info] + got)
    for n in range(len(LEGS) // 2):
        halo = lax.ppermute(halo, AXES, leg(n))

    for axis, bit, _ in DOUBLING:
        spread = jnp.concatenate([spread, send(spread, flip(axis, bit))])
    quarter = jnp.broadcast_to(part[None, :, :, : 2 * DIM], (YS, WINDOWS, PART, 2 * DIM))
    quarters = lax.all_to_all(quarter, ("zq", "core"), 0, 0)
    asked = [asked[0]] + [send(asked[d], flip("y", d)) for d in range(1, YS)]
    halo, quarters, spread, asked = tie((halo, quarters, spread, asked))

    for n in range(len(LEGS) // 2, len(LEGS)):
        halo = lax.ppermute(halo, AXES, leg(n))
    far = call(far_kernel, (WINDOWS, PART, 2 * DIM), 10**9, [part, quarters])
    far = lax.all_to_all(far, GRP, 0, 0).reshape(YS, BLOCK, 2 * DIM)
    summary = [spread] + [send(spread, flip("x", d)) for d in range(1, XS)]
    halo, far, summary = tie((halo, far, summary))

    out = call(
        attend_kernel,
        (YS, BLOCK, WIDE + DIM),
        2 * 10**9,
        [info, fixed_ok] + got + asked + [halo] + summary,
        [pltpu.VMEM((YS, ROWS, WIDE), bf16), pltpu.VMEM((YS, BLOCK, WIDE), bf16)],
    )
    back = lax.all_to_all(out, "y", 0, 0)
    return call(merge_kernel, queries.shape, 10**6, [back, far])


def solution(mesh):
    fine = Mesh(mesh.devices.reshape(tuple(SIZES.values())), AXES)
    return jax.shard_map(
        on_device,
        mesh=fine,
        in_specs=(P(AXES, None), P(AXES, None), P(AXES, None), P(AXES), P()),
        out_specs=P(AXES, None),
        check_vma=False,
    )
```

```python
import itertools
import math

import jax
import jax.numpy as jnp
from jax import lax
from jax.experimental import pallas as pl
from jax.experimental.pallas import tpu as pltpu
from jax.sharding import Mesh, PartitionSpec as P

HEADS = 24
DIM = 128
BLOCK = 128
LOCAL = 16
ZP, ZQ, CORES, XS, ZH, YS = 4, 2, 2, 4, 2, 4
AXES = ("zp", "zq", "core", "x", "zh", "y")
SIZES = dict(zip(AXES, (ZP, ZQ, CORES, XS, ZH, YS)))
GRP = ("zp", "zq", "core")
WINDOWS = ZP * ZQ * CORES
PART = BLOCK // YS
PER = LOCAL // YS
MINE = PER + 2
WIDE = MINE * DIM
ROWS = 2 * BLOCK + 16
MARK = 128.0
NEG = -1e30
LEGS = (2, 2, 4)
LEAST = -1e4
SCALE = 1.0 / (math.sqrt(DIM) * math.log(2.0))
f32, bf16 = jnp.float32, jnp.bfloat16


def index_of(place):
    at = 0
    for axis in AXES:
        at = at * SIZES[axis] + place[axis]
    return at


def route(move):
    pairs = []
    for spot in itertools.product(*(range(SIZES[a]) for a in AXES)):
        place = dict(zip(AXES, spot))
        to = move(place)
        if to is not None:
            pairs.append((index_of(place), index_of({**place, **to})))
    return pairs


def send(value, move):
    return lax.ppermute(value, AXES, route(move))


def next_group(p):
    if p["zh"] == 0:
        return dict(p, zh=1)
    if p["x"] < XS - 1:
        return dict(p, zh=0, x=p["x"] + 1)
    window = (p["zp"] * ZQ + p["zq"]) * CORES + p["core"] + 1
    if window == WINDOWS:
        return None
    return dict(p, zh=0, x=0, zp=window // (ZQ * CORES), zq=window // CORES % ZQ, core=window % CORES)


def along_z(p, steps):
    z = (p["zh"] * ZP + p["zp"]) * ZQ + p["zq"]
    z = (z + (steps if p["core"] == 0 else -steps)) % (ZH * ZP * ZQ)
    return dict(p, zh=z // (ZP * ZQ), zp=z // ZQ % ZP, zq=z % ZQ)


def leg(n):
    pairs = []
    for spot in itertools.product(*(range(SIZES[a]) for a in AXES)):
        place = dict(zip(AXES, spot))
        end = next_group(place)
        if end is not None:
            to = along_z(place, sum(LEGS[: n + 1])) if n < len(LEGS) - 1 else end
            pairs.append((index_of(along_z(place, sum(LEGS[:n]))), index_of(to)))
    return pairs


def flip(axis, bits):
    return lambda p: {axis: p[axis] ^ bits}


def heads_of(y):
    return [PER * y + i for i in range(PER)] + [LOCAL + y, LOCAL + YS + y]


def qk(a, b):
    return lax.dot_general(a, b, (((1,), (1,)), ((), ())), preferred_element_type=f32)


def pv(p, v):
    return jnp.dot(p.astype(bf16), v, preferred_element_type=f32)


def unmarked(keys):
    rows = 16
    pick = jnp.where(lax.broadcasted_iota(jnp.int32, (rows, DIM), 1) == 0, 1.0, 0.0).astype(bf16)
    return qk(pick, keys)[0:1] < MARK / 2


def column(head):
    return slice(head * DIM, (head + 1) * DIM)


def fetch(pairs, sems):
    copies = [pltpu.make_async_copy(a, b, sems.at[n]) for n, (a, b) in enumerate(pairs)]
    for copy in copies:
        copy.start()
    for copy in copies:
        copy.wait()


def keep_of(row):
    return jnp.transpose(jnp.broadcast_to(row.astype(f32), (BLOCK, DIM))) > 0.5


def pack_kernel(info, keep_row, q_in, k_in, v_in, s1, f1, *outs):
    pieces, queries, (q, k, v, sems) = outs[:YS], outs[YS : 2 * YS], outs[2 * YS :]
    fetch([(q_in, q), (k_in, k), (v_in, v)], sems)
    keep = keep_of(keep_row[...])
    for h in range(YS):
        c = column(LOCAL + YS + h)
        key = jnp.where(keep, k[:, c], jnp.array(MARK, bf16))
        for s in range(BLOCK // PART):
            r = slice(s * PART, (s + 1) * PART)
            s1[h * YS + s, :, 0:DIM] = key[r]
            s1[h * YS + s, :, DIM : 2 * DIM] = v[r, c]
            s1[h * YS + s, :, 2 * DIM : 3 * DIM] = q[r, c]
        c = column(LOCAL + h)
        key = jnp.where(keep, k[:, c], jnp.array(MARK, bf16))
        for s in range(XS):
            r = slice(s * PART, (s + 1) * PART)
            f1[s * YS + h, :, 0:DIM] = key[r]
            f1[s * YS + h, :, DIM : 2 * DIM] = v[r, c]
    row = jnp.broadcast_to(keep_row[...].astype(f32), (16, BLOCK)).astype(bf16)
    for here in range(YS):

        @pl.when(info[1] == here)
        def _():
            for d in range(YS):
                for i, h in enumerate(heads_of(here ^ d)):
                    to = column(i)
                    pieces[d][0:BLOCK, to] = k[:, column(h)]
                    pieces[d][BLOCK : 2 * BLOCK, to] = v[:, column(h)]
                    pieces[d][2 * BLOCK : ROWS, to] = row
                    queries[d][:, to] = q[:, column(h)]


def halo_kernel(info, r0, r1, r2, r3, out):
    refs = (r0, r1, r2, r3)
    for here in range(YS):

        @pl.when(info[1] == here)
        def _():
            for i in range(2):
                ref = refs[here ^ (2 + i)]
                keep = keep_of(ref[2 * BLOCK : 2 * BLOCK + 1, 0:BLOCK])
                for h in range(MINE):
                    c = column(h)
                    out[i, 0:BLOCK, c] = jnp.where(keep, ref[0:BLOCK, c], jnp.array(MARK, bf16))
                out[i, BLOCK : 2 * BLOCK] = ref[BLOCK : 2 * BLOCK]


def stats_of(top, total, shape):
    rough = total.astype(bf16).astype(f32)
    lanes = lax.broadcasted_iota(jnp.int32, shape, 1)
    return jnp.where(lanes == 0, top, jnp.where(lanes == 1, rough, total - rough)).astype(bf16)


def far_kernel(part, keys_values, out):
    count = WINDOWS * BLOCK
    kv = keys_values[...].reshape(count, 2 * DIM)
    flags = unmarked(kv[:, :DIM])
    step = 128
    for t in range(WINDOWS * PART // step):
        windows = step // PART
        query = part[t * windows : (t + 1) * windows, :, 2 * DIM : 3 * DIM].reshape(step, DIM)
        row_window = t * windows + lax.broadcasted_iota(jnp.int32, (step, count), 0) // PART
        key_window = lax.broadcasted_iota(jnp.int32, (step, count), 1) // PART % WINDOWS
        ok = (key_window < row_window) & jnp.broadcast_to(flags, (step, count))
        scores = jnp.where(ok, qk(query, kv[:, :DIM]) * SCALE, NEG)
        top = jnp.maximum(jnp.max(scores, axis=1, keepdims=True), LEAST)
        top = top.astype(bf16).astype(f32)
        weights = jnp.exp2(scores - top)
        total = jnp.sum(weights, axis=1, keepdims=True)
        acc = pv(weights, kv[:, DIM:])
        both = jnp.concatenate([acc.astype(bf16), stats_of(top, total, (step, DIM))], axis=1)
        out[t * windows : (t + 1) * windows] = both.reshape(windows, PART, 2 * DIM)


def attend(info, work, kv, q, halo, summary, fixed_ok, out, first=0):
    rows = lax.broadcasted_iota(jnp.int32, (BLOCK, BLOCK), 0)
    cols = lax.broadcasted_iota(jnp.int32, (BLOCK, BLOCK), 1)
    keeps = [kv[j, 2 * BLOCK : 2 * BLOCK + 1, 0:BLOCK].astype(f32) > 0.5 for j in range(YS)]
    far_flags = [unmarked(f[:, 0:DIM]) for f in summary]
    if halo is not None:
        halo_keeps = [unmarked(halo[i, 0:BLOCK, 0:DIM]) & (info[0] > 0) for i in range(2)]
    for j in range(YS):
        heads = [h for jj, h in work if jj == j]
        if not heads:
            continue
        masks = [((cols <= rows) & jnp.broadcast_to(keeps[j], (BLOCK, BLOCK))) | (cols == rows)]
        for back in (1, 2):
            flag = keeps[j - back] if j >= back else halo_keeps[2 + j - back]
            masks.append(jnp.broadcast_to(flag, (BLOCK, BLOCK)))
        all_scores, all_values = [], []
        for h in heads:
            c = column(h)
            query = q[j, :, c]
            scores, values = [], []
            for back in range(3):
                ref, at = (kv, j - back) if j >= back else (halo, 2 + j - back)
                scores.append(jnp.where(masks[back], qk(query, ref[at, 0:BLOCK, c]) * SCALE, NEG))
                values.append(ref[at, BLOCK : 2 * BLOCK, c])
            if h == PER:
                for f, flag in zip(summary, far_flags):
                    ok = flag & (fixed_ok[j : j + 1, :] > 0.5)
                    s = qk(query, f[:, 0:DIM]) * SCALE
                    scores.append(jnp.where(jnp.broadcast_to(ok, s.shape), s, NEG))
                    values.append(f[:, DIM : 2 * DIM])
            all_scores.append(scores)
            all_values.append(values)
        tops = []
        for h, scores in zip(heads, all_scores):
            top = jnp.max(jnp.maximum(jnp.maximum(scores[0], scores[1]), scores[2]), axis=1, keepdims=True)
            for s in scores[3:]:
                top = jnp.maximum(top, jnp.max(s, axis=1, keepdims=True))
            tops.append(top.astype(bf16).astype(f32) if h == PER + 1 else top)
        all_weights = [[jnp.exp2(s - top) for s in scores] for scores, top in zip(all_scores, tops)]
        totals, accs = [], []
        for weights, values in zip(all_weights, all_values):
            total = jnp.sum(weights[0] + weights[1] + weights[2], axis=1, keepdims=True)
            acc = pv(weights[0], values[0]) + pv(weights[1], values[1]) + pv(weights[2], values[2])
            for w, v in zip(weights[3:], values[3:]):
                total = total + jnp.sum(w, axis=1, keepdims=True)
                acc = acc + pv(w, v)
            totals.append(total)
            accs.append(acc)
        for h, top, total, acc in zip(heads, tops, totals, accs):
            c = column(h)
            if h == PER + 1:
                out[j - first, :, c] = acc.astype(bf16)
                out[j - first, :, column(h + 1)] = stats_of(top, total, (BLOCK, DIM))
            else:
                out[j - first, :, c] = (acc / total).astype(bf16)


def by_block(info, pieces, queries, kv, q):
    here = info[1]
    return [(a, kv.at[here ^ d]) for d, a in enumerate(pieces)] + [(a, q.at[here ^ d]) for d, a in enumerate(queries)]


EARLY = [(j, h) for j in (2, 3) for h in range(MINE)]
LATE = [(j, h) for j in (0, 1) for h in range(MINE)]


def gather(info, p, q_in, f_in, kv, q, f, sems):
    pairs = by_block(info, p, q_in, kv, q) + [(a, f.at[d]) for d, a in enumerate(f_in)]
    fetch(pairs, sems)
    return [f.at[d] for d in range(XS)]


def early_kernel(info, fixed_ok, p0, p1, p2, p3, q0, q1, q2, q3, f0, f1, f2, f3, out, kv, q, f, sems):
    summary = gather(info, (p0, p1, p2, p3), (q0, q1, q2, q3), (f0, f1, f2, f3), kv, q, f, sems)
    attend(info, EARLY, kv, q, None, summary, fixed_ok, out, first=2)


def late_kernel(info, fixed_ok, halo, early, p0, p1, p2, p3, q0, q1, q2, q3, f0, f1, f2, f3, out, kv, q, f, sems):
    summary = gather(info, (p0, p1, p2, p3), (q0, q1, q2, q3), (f0, f1, f2, f3), kv, q, f, sems)
    attend(info, LATE, kv, q, halo, summary, fixed_ok, out)
    out[2:YS] = early[...]


def merge_kernel(back, far, out):
    for y in range(YS):
        for i, h in enumerate(heads_of(y)[:-1]):
            out[:, column(h)] = back[y, :, column(i)]
        near = back[y, :, column(MINE)].astype(f32)
        there = far[y, :, column(1)].astype(f32)
        near_top, near_total = near[:, 0:1], near[:, 1:2] + near[:, 2:3]
        far_top, far_total = there[:, 0:1], there[:, 1:2] + there[:, 2:3]
        top = jnp.maximum(near_top, far_top)
        near_scale, far_scale = jnp.exp2(near_top - top), jnp.exp2(far_top - top)
        acc = back[y, :, column(MINE - 1)].astype(f32) * near_scale
        acc = acc + far[y, :, column(0)].astype(f32) * far_scale
        total = near_total * near_scale + far_total * far_scale
        out[:, column(heads_of(y)[-1])] = (acc / total).astype(bf16)


VMEM = pl.BlockSpec(memory_space=pltpu.VMEM)
SMEM = pl.BlockSpec(memory_space=pltpu.SMEM)


ANY = pl.BlockSpec(memory_space=pl.ANY)


def call(kernel, shapes, flops, operands, scratch=(), left=0):
    many = isinstance(shapes, list)
    moved = sum(o.size * o.dtype.itemsize for o in operands)
    outs = [jax.ShapeDtypeStruct(s, bf16) for s in shapes] if many else jax.ShapeDtypeStruct(shapes, bf16)
    return pl.pallas_call(
        kernel,
        out_shape=outs,
        in_specs=[SMEM if o.ndim == 1 else VMEM for o in operands[: len(operands) - left]] + [ANY] * left,
        out_specs=[VMEM] * len(shapes) if many else VMEM,
        scratch_shapes=scratch,
        compiler_params=pltpu.CompilerParams(vmem_limit_bytes=(58 if left else 40) << 20),
        cost_estimate=pl.CostEstimate(flops=flops, bytes_accessed=moved, transcendentals=0),
        name=kernel.__name__,
    )(*operands)


tie = lax.optimization_barrier


def on_device(queries, key_states, value_states, key_keep, summary_pos):
    zp, zq, core, x, zh, y = (lax.axis_index(a) for a in AXES)
    window = (zp * ZQ + zq) * CORES + core
    group = window * (XS * ZH) + x * ZH + zh
    info = jnp.stack([(group > 0).astype(jnp.int32), y.astype(jnp.int32)])

    windows = jnp.arange(WINDOWS, dtype=jnp.int32)
    block_ids = group * YS + jnp.arange(YS, dtype=jnp.int32)
    fixed_ok = (windows * (XS * ZH * YS) + summary_pos)[None, :] < block_ids[:, None] - 2
    fixed_ok = jnp.repeat(fixed_ok.astype(f32), PART, axis=1)

    shapes = [(WINDOWS, PART, 3 * DIM), (XS * YS, PART, 2 * DIM)] + [(ROWS, WIDE)] * YS + [(BLOCK, WIDE)] * YS
    wide = pltpu.VMEM((BLOCK, HEADS * DIM), bf16)
    scratch = [wide, wide, wide, pltpu.SemaphoreType.DMA((3,))]
    rows = [info, key_keep.reshape(1, BLOCK), queries, key_states, value_states]
    packed = call(pack_kernel, shapes, 10**6, rows, scratch, left=3)
    s1, f1, pieces, asked = packed[0], packed[1], packed[2 : 2 + YS], packed[2 + YS :]
    root = jnp.sum(jnp.where(windows == window, summary_pos, 0))
    slot = jnp.arange(XS * YS, dtype=jnp.int32) == root // (ZH * YS) * YS + root % YS
    here = zh == root // YS % ZH

    got = [pieces[0]] + [send(pieces[d], flip("y", d)) for d in range(1, YS)]
    parts = lax.all_to_all(f1, ("x", "y"), 0, 0)
    parts, s1 = tie((parts, s1))
    part = lax.all_to_all(s1, GRP, 0, 0)
    piece = jnp.sum(jnp.where(slot[:, None, None], parts, 0).astype(f32), axis=0).astype(bf16)
    twin = send(piece, flip("zh", 1))
    spread = jnp.where(here, piece, twin)
    got1, got2, got3, part, spread = tie((got[1], got[2], got[3], part, spread))
    got = [got[0], got1, got2, got3]

    quarter = jnp.broadcast_to(part[None, :, :, : 2 * DIM], (YS, WINDOWS, PART, 2 * DIM))
    quarters = lax.all_to_all(quarter, ("zq", "core"), 0, 0)
    halo = call(halo_kernel, (2, 2 * BLOCK, WIDE), 10**6, [info] + got)
    halo = lax.ppermute(halo, AXES, leg(0))
    halo, quarters, spread = tie((halo, quarters, spread))
    halo = lax.ppermute(halo, AXES, leg(1))
    spread = jnp.broadcast_to(spread[None], (WINDOWS,) + spread.shape)
    spread = lax.all_to_all(spread, GRP, 0, 0).reshape(-1, 2 * DIM)
    part, halo = tie((part, halo))
    far = call(far_kernel, (WINDOWS, PART, 2 * DIM), 10**10, [part, quarters])
    halo, far, spread, asked = tie((halo, far, spread, asked))

    halo = lax.ppermute(halo, AXES, leg(2))
    asked = [asked[0]] + [send(asked[d], flip("y", d)) for d in range(1, YS)]
    scratch = [
        pltpu.VMEM((YS, ROWS, WIDE), bf16),
        pltpu.VMEM((YS, BLOCK, WIDE), bf16),
        pltpu.VMEM((XS, WINDOWS * PART, 2 * DIM), bf16),
        pltpu.SemaphoreType.DMA((2 * YS + XS,)),
    ]
    shape = (YS, BLOCK, WIDE + DIM)
    far = lax.all_to_all(far, GRP, 0, 0).reshape(YS, BLOCK, 2 * DIM)
    summary = [spread] + [send(spread, flip("x", d)) for d in range(1, XS)]
    rest = got + asked + summary
    early = call(early_kernel, (2,) + shape[1:], 3 * 10**8, [info, fixed_ok] + rest, scratch, left=len(rest))
    halo, early = tie((halo, early))
    out = call(late_kernel, shape, 10**10, [info, fixed_ok, halo, early] + rest, scratch, left=len(rest))
    out, far = tie((out, far))
    back = lax.all_to_all(out, "y", 0, 0)
    return call(merge_kernel, queries.shape, 10**6, [back, far])


def solution(mesh):
    fine = Mesh(mesh.devices.reshape(tuple(SIZES.values())), AXES)
    return jax.shard_map(
        on_device,
        mesh=fine,
        in_specs=(P(AXES, None), P(AXES, None), P(AXES, None), P(AXES), P()),
        out_specs=P(AXES, None),
        check_vma=False,
    )
```

```python
import itertools
import math

import jax
import jax.numpy as jnp
from jax import lax
from jax.experimental import pallas as pl
from jax.experimental.pallas import tpu as pltpu
from jax.sharding import Mesh, PartitionSpec as P

HEADS = 24
DIM = 128
BLOCK = 128
LOCAL = 16
ZP, ZQ, CORES, XS, ZH, YS = 4, 2, 2, 4, 2, 4
AXES = ("zp", "zq", "core", "x", "zh", "y")
SIZES = dict(zip(AXES, (ZP, ZQ, CORES, XS, ZH, YS)))
GRP = ("zp", "zq", "core")
WINDOWS = ZP * ZQ * CORES
PART = BLOCK // YS
PER = LOCAL // YS
MINE = PER + 2
WIDE = MINE * DIM
ROWS = 2 * BLOCK + 16
MARK = 128.0
NEG = -1e30
LEGS = (2, 3, 3)
LEAST = -1e4
SCALE = 1.0 / (math.sqrt(DIM) * math.log(2.0))
f32, bf16 = jnp.float32, jnp.bfloat16


def index_of(place):
    at = 0
    for axis in AXES:
        at = at * SIZES[axis] + place[axis]
    return at


def route(move):
    pairs = []
    for spot in itertools.product(*(range(SIZES[a]) for a in AXES)):
        place = dict(zip(AXES, spot))
        to = move(place)
        if to is not None:
            pairs.append((index_of(place), index_of({**place, **to})))
    return pairs


def send(value, move):
    return lax.ppermute(value, AXES, route(move))


def next_group(p):
    if p["zh"] == 0:
        return dict(p, zh=1)
    if p["x"] < XS - 1:
        return dict(p, zh=0, x=p["x"] + 1)
    window = (p["zp"] * ZQ + p["zq"]) * CORES + p["core"] + 1
    if window == WINDOWS:
        return None
    return dict(p, zh=0, x=0, zp=window // (ZQ * CORES), zq=window // CORES % ZQ, core=window % CORES)


def along_z(p, steps):
    z = (p["zh"] * ZP + p["zp"]) * ZQ + p["zq"]
    z = (z + (steps if p["core"] == 0 else -steps)) % (ZH * ZP * ZQ)
    return dict(p, zh=z // (ZP * ZQ), zp=z // ZQ % ZP, zq=z % ZQ)


def leg(n):
    pairs = []
    for spot in itertools.product(*(range(SIZES[a]) for a in AXES)):
        place = dict(zip(AXES, spot))
        end = next_group(place)
        if end is not None:
            to = along_z(place, sum(LEGS[: n + 1])) if n < len(LEGS) - 1 else end
            pairs.append((index_of(along_z(place, sum(LEGS[:n]))), index_of(to)))
    return pairs


def flip(axis, bits):
    return lambda p: {axis: p[axis] ^ bits}


def heads_of(y):
    return [PER * y + i for i in range(PER)] + [LOCAL + y, LOCAL + YS + y]


def qk(a, b):
    return lax.dot_general(a, b, (((1,), (1,)), ((), ())), preferred_element_type=f32)


def pv(p, v):
    return jnp.dot(p.astype(bf16), v, preferred_element_type=f32)


def unmarked(keys):
    rows = 16
    pick = jnp.where(lax.broadcasted_iota(jnp.int32, (rows, DIM), 1) == 0, 1.0, 0.0).astype(bf16)
    return qk(pick, keys)[0:1] < MARK / 2


def column(head):
    return slice(head * DIM, (head + 1) * DIM)


def fetch(pairs, sems):
    copies = [pltpu.make_async_copy(a, b, sems.at[n]) for n, (a, b) in enumerate(pairs)]
    for copy in copies:
        copy.start()
    for copy in copies:
        copy.wait()


def keep_of(row):
    return jnp.transpose(jnp.broadcast_to(row.astype(f32), (BLOCK, DIM))) > 0.5


def pack_kernel(info, keep_row, q_in, k_in, v_in, s1, f1, *outs):
    pieces, queries, (q, k, v, sems) = outs[:YS], outs[YS : 2 * YS], outs[2 * YS :]
    fetch([(q_in, q), (k_in, k), (v_in, v)], sems)
    keep = keep_of(keep_row[...])
    for h in range(YS):
        c = column(LOCAL + YS + h)
        key = jnp.where(keep, k[:, c], jnp.array(MARK, bf16))
        for s in range(BLOCK // PART):
            r = slice(s * PART, (s + 1) * PART)
            s1[h * YS + s, :, 0:DIM] = key[r]
            s1[h * YS + s, :, DIM : 2 * DIM] = v[r, c]
            s1[h * YS + s, :, 2 * DIM : 3 * DIM] = q[r, c]
        c = column(LOCAL + h)
        key = jnp.where(keep, k[:, c], jnp.array(MARK, bf16))
        for s in range(XS):
            r = slice(s * PART, (s + 1) * PART)
            f1[s * YS + h, :, 0:DIM] = key[r]
            f1[s * YS + h, :, DIM : 2 * DIM] = v[r, c]
    row = jnp.broadcast_to(keep_row[...].astype(f32), (16, BLOCK)).astype(bf16)
    for here in range(YS):

        @pl.when(info[1] == here)
        def _():
            for d in range(YS):
                for i, h in enumerate(heads_of(here ^ d)):
                    to = column(i)
                    pieces[d][0:BLOCK, to] = k[:, column(h)]
                    pieces[d][BLOCK : 2 * BLOCK, to] = v[:, column(h)]
                    pieces[d][2 * BLOCK : ROWS, to] = row
                    queries[d][:, to] = q[:, column(h)]


def halo_kernel(info, r0, r1, r2, r3, out):
    refs = (r0, r1, r2, r3)
    for here in range(YS):

        @pl.when(info[1] == here)
        def _():
            for i in range(2):
                ref = refs[here ^ (2 + i)]
                keep = keep_of(ref[2 * BLOCK : 2 * BLOCK + 1, 0:BLOCK])
                for h in range(MINE):
                    c = column(h)
                    out[i, 0:BLOCK, c] = jnp.where(keep, ref[0:BLOCK, c], jnp.array(MARK, bf16))
                out[i, BLOCK : 2 * BLOCK] = ref[BLOCK : 2 * BLOCK]


def stats_of(top, total, shape):
    rough = total.astype(bf16).astype(f32)
    lanes = lax.broadcasted_iota(jnp.int32, shape, 1)
    return jnp.where(lanes == 0, top, jnp.where(lanes == 1, rough, total - rough)).astype(bf16)


def far_kernel(part, keys_values, out):
    count = WINDOWS * BLOCK
    kv = keys_values[...].reshape(count, 2 * DIM)
    flags = unmarked(kv[:, :DIM])
    step = 128
    for t in range(WINDOWS * PART // step):
        windows = step // PART
        query = part[t * windows : (t + 1) * windows, :, 2 * DIM : 3 * DIM].reshape(step, DIM)
        row_window = t * windows + lax.broadcasted_iota(jnp.int32, (step, count), 0) // PART
        key_window = lax.broadcasted_iota(jnp.int32, (step, count), 1) // PART % WINDOWS
        ok = (key_window < row_window) & jnp.broadcast_to(flags, (step, count))
        scores = jnp.where(ok, qk(query, kv[:, :DIM]) * SCALE, NEG)
        top = jnp.maximum(jnp.max(scores, axis=1, keepdims=True), LEAST)
        top = top.astype(bf16).astype(f32)
        weights = jnp.exp2(scores - top)
        total = jnp.sum(weights, axis=1, keepdims=True)
        acc = pv(weights, kv[:, DIM:])
        both = jnp.concatenate([acc.astype(bf16), stats_of(top, total, (step, DIM))], axis=1)
        out[t * windows : (t + 1) * windows] = both.reshape(windows, PART, 2 * DIM)


def attend(info, work, kv, q, halo, summary, fixed_ok, out, first=0):
    rows = lax.broadcasted_iota(jnp.int32, (BLOCK, BLOCK), 0)
    cols = lax.broadcasted_iota(jnp.int32, (BLOCK, BLOCK), 1)
    keeps = [kv[j, 2 * BLOCK : 2 * BLOCK + 1, 0:BLOCK].astype(f32) > 0.5 for j in range(YS)]
    far_flags = [unmarked(f[:, 0:DIM]) for f in summary]
    if halo is not None:
        halo_keeps = [unmarked(halo[i, 0:BLOCK, 0:DIM]) & (info[0] > 0) for i in range(2)]
    for j in range(YS):
        heads = [h for jj, h in work if jj == j]
        if not heads:
            continue
        masks = [((cols <= rows) & jnp.broadcast_to(keeps[j], (BLOCK, BLOCK))) | (cols == rows)]
        for back in (1, 2):
            flag = keeps[j - back] if j >= back else halo_keeps[2 + j - back]
            masks.append(jnp.broadcast_to(flag, (BLOCK, BLOCK)))
        all_scores, all_values = [], []
        for h in heads:
            c = column(h)
            query = q[j, :, c]
            scores, values = [], []
            for back in range(3):
                ref, at = (kv, j - back) if j >= back else (halo, 2 + j - back)
                scores.append(jnp.where(masks[back], qk(query, ref[at, 0:BLOCK, c]) * SCALE, NEG))
                values.append(ref[at, BLOCK : 2 * BLOCK, c])
            if h == PER:
                for f, flag in zip(summary, far_flags):
                    ok = flag & (fixed_ok[j : j + 1, :] > 0.5)
                    s = qk(query, f[:, 0:DIM]) * SCALE
                    scores.append(jnp.where(jnp.broadcast_to(ok, s.shape), s, NEG))
                    values.append(f[:, DIM : 2 * DIM])
            all_scores.append(scores)
            all_values.append(values)
        tops = []
        for h, scores in zip(heads, all_scores):
            top = jnp.max(jnp.maximum(jnp.maximum(scores[0], scores[1]), scores[2]), axis=1, keepdims=True)
            for s in scores[3:]:
                top = jnp.maximum(top, jnp.max(s, axis=1, keepdims=True))
            tops.append(top.astype(bf16).astype(f32) if h == PER + 1 else top)
        all_weights = [[jnp.exp2(s - top) for s in scores] for scores, top in zip(all_scores, tops)]
        totals, accs = [], []
        for weights, values in zip(all_weights, all_values):
            total = jnp.sum(weights[0] + weights[1] + weights[2], axis=1, keepdims=True)
            acc = pv(weights[0], values[0]) + pv(weights[1], values[1]) + pv(weights[2], values[2])
            for w, v in zip(weights[3:], values[3:]):
                total = total + jnp.sum(w, axis=1, keepdims=True)
                acc = acc + pv(w, v)
            totals.append(total)
            accs.append(acc)
        for h, top, total, acc in zip(heads, tops, totals, accs):
            c = column(h)
            if h == PER + 1:
                out[j - first, :, c] = acc.astype(bf16)
                out[j - first, :, column(h + 1)] = stats_of(top, total, (BLOCK, DIM))
            else:
                out[j - first, :, c] = (acc / total).astype(bf16)


def by_block(info, pieces, queries, kv, q):
    here = info[1]
    return [(a, kv.at[here ^ d]) for d, a in enumerate(pieces)] + [(a, q.at[here ^ d]) for d, a in enumerate(queries)]


EARLY = [(j, h) for j in (2, 3) for h in range(MINE)]
LATE = [(j, h) for j in (0, 1) for h in range(MINE)]


def gather(info, p, q_in, f_in, kv, q, f, sems):
    pairs = by_block(info, p, q_in, kv, q) + [(a, f.at[d]) for d, a in enumerate(f_in)]
    fetch(pairs, sems)
    return [f.at[d] for d in range(XS)]


def early_kernel(info, fixed_ok, p0, p1, p2, p3, q0, q1, q2, q3, f0, f1, f2, f3, out, kv, q, f, sems):
    summary = gather(info, (p0, p1, p2, p3), (q0, q1, q2, q3), (f0, f1, f2, f3), kv, q, f, sems)
    attend(info, EARLY, kv, q, None, summary, fixed_ok, out, first=2)


def late_kernel(info, fixed_ok, halo, early, p0, p1, p2, p3, q0, q1, q2, q3, f0, f1, f2, f3, out, kv, q, f, sems):
    summary = gather(info, (p0, p1, p2, p3), (q0, q1, q2, q3), (f0, f1, f2, f3), kv, q, f, sems)
    attend(info, LATE, kv, q, halo, summary, fixed_ok, out)
    out[2:YS] = early[...]


def merge_kernel(back, far, out):
    for y in range(YS):
        for i, h in enumerate(heads_of(y)[:-1]):
            out[:, column(h)] = back[y, :, column(i)]
        near = back[y, :, column(MINE)].astype(f32)
        there = far[y, :, column(1)].astype(f32)
        near_top, near_total = near[:, 0:1], near[:, 1:2] + near[:, 2:3]
        far_top, far_total = there[:, 0:1], there[:, 1:2] + there[:, 2:3]
        top = jnp.maximum(near_top, far_top)
        near_scale, far_scale = jnp.exp2(near_top - top), jnp.exp2(far_top - top)
        acc = back[y, :, column(MINE - 1)].astype(f32) * near_scale
        acc = acc + far[y, :, column(0)].astype(f32) * far_scale
        total = near_total * near_scale + far_total * far_scale
        out[:, column(heads_of(y)[-1])] = (acc / total).astype(bf16)


VMEM = pl.BlockSpec(memory_space=pltpu.VMEM)
SMEM = pl.BlockSpec(memory_space=pltpu.SMEM)


ANY = pl.BlockSpec(memory_space=pl.ANY)


def call(kernel, shapes, flops, operands, scratch=(), left=0):
    many = isinstance(shapes, list)
    moved = sum(o.size * o.dtype.itemsize for o in operands)
    outs = [jax.ShapeDtypeStruct(s, bf16) for s in shapes] if many else jax.ShapeDtypeStruct(shapes, bf16)
    return pl.pallas_call(
        kernel,
        out_shape=outs,
        in_specs=[SMEM if o.ndim == 1 else VMEM for o in operands[: len(operands) - left]] + [ANY] * left,
        out_specs=[VMEM] * len(shapes) if many else VMEM,
        scratch_shapes=scratch,
        compiler_params=pltpu.CompilerParams(vmem_limit_bytes=(58 if left else 40) << 20),
        cost_estimate=pl.CostEstimate(flops=flops, bytes_accessed=moved, transcendentals=0),
        name=kernel.__name__,
    )(*operands)


tie = lax.optimization_barrier


def on_device(queries, key_states, value_states, key_keep, summary_pos):
    zp, zq, core, x, zh, y = (lax.axis_index(a) for a in AXES)
    window = (zp * ZQ + zq) * CORES + core
    group = window * (XS * ZH) + x * ZH + zh
    info = jnp.stack([(group > 0).astype(jnp.int32), y.astype(jnp.int32)])

    windows = jnp.arange(WINDOWS, dtype=jnp.int32)
    block_ids = group * YS + jnp.arange(YS, dtype=jnp.int32)
    fixed_ok = (windows * (XS * ZH * YS) + summary_pos)[None, :] < block_ids[:, None] - 2
    fixed_ok = jnp.repeat(fixed_ok.astype(f32), PART, axis=1)

    shapes = [(WINDOWS, PART, 3 * DIM), (XS * YS, PART, 2 * DIM)] + [(ROWS, WIDE)] * YS + [(BLOCK, WIDE)] * YS
    wide = pltpu.VMEM((BLOCK, HEADS * DIM), bf16)
    scratch = [wide, wide, wide, pltpu.SemaphoreType.DMA((3,))]
    rows = [info, key_keep.reshape(1, BLOCK), queries, key_states, value_states]
    packed = call(pack_kernel, shapes, 10**6, rows, scratch, left=3)
    s1, f1, pieces, asked = packed[0], packed[1], packed[2 : 2 + YS], packed[2 + YS :]
    root = jnp.sum(jnp.where(windows == window, summary_pos, 0))
    slot = jnp.arange(XS * YS, dtype=jnp.int32) == root // (ZH * YS) * YS + root % YS
    here = zh == root // YS % ZH

    got = [pieces[0]] + [send(pieces[d], flip("y", d)) for d in range(1, YS)]
    parts = lax.all_to_all(f1, ("x", "y"), 0, 0)
    parts, s1 = tie((parts, s1))
    part = lax.all_to_all(s1, GRP, 0, 0)
    piece = jnp.sum(jnp.where(slot[:, None, None], parts, 0).astype(f32), axis=0).astype(bf16)
    twin = send(piece, flip("zh", 1))
    spread = jnp.where(here, piece, twin)
    got1, got2, got3, part, spread = tie((got[1], got[2], got[3], part, spread))
    got = [got[0], got1, got2, got3]

    quarter = jnp.broadcast_to(part[None, :, :, : 2 * DIM], (YS, WINDOWS, PART, 2 * DIM))
    quarters = lax.all_to_all(quarter, ("zq", "core"), 0, 0)
    halo = call(halo_kernel, (2, 2 * BLOCK, WIDE), 10**6, [info] + got)
    halo = lax.ppermute(halo, AXES, leg(0))
    halo, quarters, spread = tie((halo, quarters, spread))
    halo = lax.ppermute(halo, AXES, leg(1))
    spread = jnp.broadcast_to(spread[None], (WINDOWS,) + spread.shape)
    spread = lax.all_to_all(spread, GRP, 0, 0).reshape(-1, 2 * DIM)
    part, halo = tie((part, halo))
    far = call(far_kernel, (WINDOWS, PART, 2 * DIM), 10**10, [part, quarters])
    asked = [asked[0]] + [send(asked[d], flip("y", d)) for d in range(1, YS)]
    halo, far, spread, asked = tie((halo, far, spread, asked))

    halo = lax.ppermute(halo, AXES, leg(2))
    scratch = [
        pltpu.VMEM((YS, ROWS, WIDE), bf16),
        pltpu.VMEM((YS, BLOCK, WIDE), bf16),
        pltpu.VMEM((XS, WINDOWS * PART, 2 * DIM), bf16),
        pltpu.SemaphoreType.DMA((2 * YS + XS,)),
    ]
    shape = (YS, BLOCK, WIDE + DIM)
    far = lax.all_to_all(far, GRP, 0, 0).reshape(YS, BLOCK, 2 * DIM)
    summary = [spread] + [send(spread, flip("x", d)) for d in range(1, XS)]
    rest = got + asked + summary
    early = call(early_kernel, (2,) + shape[1:], 3 * 10**8, [info, fixed_ok] + rest, scratch, left=len(rest))
    halo, early = tie((halo, early))
    out = call(late_kernel, shape, 10**10, [info, fixed_ok, halo, early] + rest, scratch, left=len(rest))
    out, far = tie((out, far))
    back = lax.all_to_all(out, "y", 0, 0)
    return call(merge_kernel, queries.shape, 10**6, [back, far])


def solution(mesh):
    fine = Mesh(mesh.devices.reshape(tuple(SIZES.values())), AXES)
    return jax.shard_map(
        on_device,
        mesh=fine,
        in_specs=(P(AXES, None), P(AXES, None), P(AXES, None), P(AXES), P()),
        out_specs=P(AXES, None),
        check_vma=False,
    )
```

```python
import itertools
import math

import jax
import jax.numpy as jnp
from jax import lax
from jax.experimental import pallas as pl
from jax.experimental.pallas import tpu as pltpu
from jax.sharding import Mesh, PartitionSpec as P

HEADS = 24
DIM = 128
BLOCK = 128
LOCAL = 16
ZP, ZQ, CORES, XS, ZH, YS = 4, 2, 2, 4, 2, 4
AXES = ("zp", "zq", "core", "x", "zh", "y")
SIZES = dict(zip(AXES, (ZP, ZQ, CORES, XS, ZH, YS)))
GRP = ("zp", "zq", "core")
WINDOWS = ZP * ZQ * CORES
PART = BLOCK // YS
PER = LOCAL // YS
MINE = PER + 2
WIDE = MINE * DIM
ROWS = 2 * BLOCK + 16
MARK = 128.0
NEG = -1e30
LEGS = (2, 3, 3)
LEAST = -1e4
SCALE = 1.0 / (math.sqrt(DIM) * math.log(2.0))
f32, bf16 = jnp.float32, jnp.bfloat16


def index_of(place):
    at = 0
    for axis in AXES:
        at = at * SIZES[axis] + place[axis]
    return at


def route(move):
    pairs = []
    for spot in itertools.product(*(range(SIZES[a]) for a in AXES)):
        place = dict(zip(AXES, spot))
        to = move(place)
        if to is not None:
            pairs.append((index_of(place), index_of({**place, **to})))
    return pairs


def send(value, move):
    return lax.ppermute(value, AXES, route(move))


def next_group(p):
    if p["zh"] == 0:
        return dict(p, zh=1)
    if p["x"] < XS - 1:
        return dict(p, zh=0, x=p["x"] + 1)
    window = (p["zp"] * ZQ + p["zq"]) * CORES + p["core"] + 1
    if window == WINDOWS:
        return None
    return dict(p, zh=0, x=0, zp=window // (ZQ * CORES), zq=window // CORES % ZQ, core=window % CORES)


def along_z(p, steps):
    z = (p["zh"] * ZP + p["zp"]) * ZQ + p["zq"]
    z = (z + (steps if p["core"] == 0 else -steps)) % (ZH * ZP * ZQ)
    return dict(p, zh=z // (ZP * ZQ), zp=z // ZQ % ZP, zq=z % ZQ)


def leg(n):
    pairs = []
    for spot in itertools.product(*(range(SIZES[a]) for a in AXES)):
        place = dict(zip(AXES, spot))
        end = next_group(place)
        if end is not None:
            to = along_z(place, sum(LEGS[: n + 1])) if n < len(LEGS) - 1 else end
            pairs.append((index_of(along_z(place, sum(LEGS[:n]))), index_of(to)))
    return pairs


def flip(axis, bits):
    return lambda p: {axis: p[axis] ^ bits}


def heads_of(y):
    return [PER * y + i for i in range(PER)] + [LOCAL + y, LOCAL + YS + y]


def qk(a, b):
    return lax.dot_general(a, b, (((1,), (1,)), ((), ())), preferred_element_type=f32)


def pv(p, v):
    return jnp.dot(p.astype(bf16), v, preferred_element_type=f32)


def unmarked(keys):
    rows = 16
    pick = jnp.where(lax.broadcasted_iota(jnp.int32, (rows, DIM), 1) == 0, 1.0, 0.0).astype(bf16)
    return qk(pick, keys)[0:1] < MARK / 2


def column(head):
    return slice(head * DIM, (head + 1) * DIM)


def fetch(pairs, sems):
    copies = [pltpu.make_async_copy(a, b, sems.at[n]) for n, (a, b) in enumerate(pairs)]
    for copy in copies:
        copy.start()
    for copy in copies:
        copy.wait()


def keep_of(row):
    return jnp.transpose(jnp.broadcast_to(row.astype(f32), (BLOCK, DIM))) > 0.5


def pack_kernel(info, keep_row, q_in, k_in, v_in, s1, f1, *outs):
    pieces, queries, (q, k, v, sems) = outs[:YS], outs[YS : 2 * YS], outs[2 * YS :]
    fetch([(q_in, q), (k_in, k), (v_in, v)], sems)
    keep = keep_of(keep_row[...])
    for h in range(YS):
        c = column(LOCAL + YS + h)
        key = jnp.where(keep, k[:, c], jnp.array(MARK, bf16))
        for s in range(BLOCK // PART):
            r = slice(s * PART, (s + 1) * PART)
            s1[h * YS + s, :, 0:DIM] = key[r]
            s1[h * YS + s, :, DIM : 2 * DIM] = v[r, c]
            s1[h * YS + s, :, 2 * DIM : 3 * DIM] = q[r, c]
        c = column(LOCAL + h)
        key = jnp.where(keep, k[:, c], jnp.array(MARK, bf16))
        for s in range(XS):
            r = slice(s * PART, (s + 1) * PART)
            f1[s * YS + h, :, 0:DIM] = key[r]
            f1[s * YS + h, :, DIM : 2 * DIM] = v[r, c]
    row = jnp.broadcast_to(keep_row[...].astype(f32), (16, BLOCK)).astype(bf16)
    for here in range(YS):

        @pl.when(info[1] == here)
        def _():
            for d in range(YS):
                for i, h in enumerate(heads_of(here ^ d)):
                    to = column(i)
                    pieces[d][0:BLOCK, to] = k[:, column(h)]
                    pieces[d][BLOCK : 2 * BLOCK, to] = v[:, column(h)]
                    pieces[d][2 * BLOCK : ROWS, to] = row
                    queries[d][:, to] = q[:, column(h)]


def halo_kernel(info, r0, r1, r2, r3, out):
    refs = (r0, r1, r2, r3)
    for here in range(YS):

        @pl.when(info[1] == here)
        def _():
            for i in range(2):
                ref = refs[here ^ (2 + i)]
                keep = keep_of(ref[2 * BLOCK : 2 * BLOCK + 1, 0:BLOCK])
                for h in range(MINE):
                    c = column(h)
                    out[i, 0:BLOCK, c] = jnp.where(keep, ref[0:BLOCK, c], jnp.array(MARK, bf16))
                out[i, BLOCK : 2 * BLOCK] = ref[BLOCK : 2 * BLOCK]


def stats_of(top, total, shape):
    rough = total.astype(bf16).astype(f32)
    lanes = lax.broadcasted_iota(jnp.int32, shape, 1)
    return jnp.where(lanes == 0, top, jnp.where(lanes == 1, rough, total - rough)).astype(bf16)


def far_kernel(part, keys_values, out):
    count = WINDOWS * BLOCK
    kv = keys_values[...].reshape(count, 2 * DIM)
    flags = unmarked(kv[:, :DIM])
    step = 128
    for t in range(WINDOWS * PART // step):
        windows = step // PART
        query = part[t * windows : (t + 1) * windows, :, 2 * DIM : 3 * DIM].reshape(step, DIM)
        row_window = t * windows + lax.broadcasted_iota(jnp.int32, (step, count), 0) // PART
        key_window = lax.broadcasted_iota(jnp.int32, (step, count), 1) // PART % WINDOWS
        ok = (key_window < row_window) & jnp.broadcast_to(flags, (step, count))
        scores = jnp.where(ok, qk(query, kv[:, :DIM]) * SCALE, NEG)
        top = jnp.maximum(jnp.max(scores, axis=1, keepdims=True), LEAST)
        top = top.astype(bf16).astype(f32)
        weights = jnp.exp2(scores - top)
        total = jnp.sum(weights, axis=1, keepdims=True)
        acc = pv(weights, kv[:, DIM:])
        both = jnp.concatenate([acc.astype(bf16), stats_of(top, total, (step, DIM))], axis=1)
        out[t * windows : (t + 1) * windows] = both.reshape(windows, PART, 2 * DIM)


def attend(info, work, kv, q, halo, summary, fixed_ok, out, first=0):
    rows = lax.broadcasted_iota(jnp.int32, (BLOCK, BLOCK), 0)
    cols = lax.broadcasted_iota(jnp.int32, (BLOCK, BLOCK), 1)
    keeps = [kv[j, 2 * BLOCK : 2 * BLOCK + 1, 0:BLOCK].astype(f32) > 0.5 for j in range(YS)]
    far_flags = [unmarked(f[:, 0:DIM]) for f in summary]
    if halo is not None:
        halo_keeps = [unmarked(halo[i, 0:BLOCK, 0:DIM]) & (info[0] > 0) for i in range(2)]
    for j in range(YS):
        heads = [h for jj, h in work if jj == j]
        if not heads:
            continue
        masks = [((cols <= rows) & jnp.broadcast_to(keeps[j], (BLOCK, BLOCK))) | (cols == rows)]
        for back in (1, 2):
            flag = keeps[j - back] if j >= back else halo_keeps[2 + j - back]
            masks.append(jnp.broadcast_to(flag, (BLOCK, BLOCK)))
        all_scores, all_values = [], []
        for h in heads:
            c = column(h)
            query = q[j, :, c]
            scores, values = [], []
            for back in range(3):
                ref, at = (kv, j - back) if j >= back else (halo, 2 + j - back)
                scores.append(jnp.where(masks[back], qk(query, ref[at, 0:BLOCK, c]) * SCALE, NEG))
                values.append(ref[at, BLOCK : 2 * BLOCK, c])
            if h == PER:
                for f, flag in zip(summary, far_flags):
                    ok = flag & (fixed_ok[j : j + 1, :] > 0.5)
                    s = qk(query, f[:, 0:DIM]) * SCALE
                    scores.append(jnp.where(jnp.broadcast_to(ok, s.shape), s, NEG))
                    values.append(f[:, DIM : 2 * DIM])
            all_scores.append(scores)
            all_values.append(values)
        tops = []
        for h, scores in zip(heads, all_scores):
            top = jnp.max(jnp.maximum(jnp.maximum(scores[0], scores[1]), scores[2]), axis=1, keepdims=True)
            for s in scores[3:]:
                top = jnp.maximum(top, jnp.max(s, axis=1, keepdims=True))
            tops.append(top.astype(bf16).astype(f32) if h == PER + 1 else top)
        all_weights = [[jnp.exp2(s - top) for s in scores] for scores, top in zip(all_scores, tops)]
        totals, accs = [], []
        for weights, values in zip(all_weights, all_values):
            total = jnp.sum(weights[0] + weights[1] + weights[2], axis=1, keepdims=True)
            acc = pv(weights[0], values[0]) + pv(weights[1], values[1]) + pv(weights[2], values[2])
            for w, v in zip(weights[3:], values[3:]):
                total = total + jnp.sum(w, axis=1, keepdims=True)
                acc = acc + pv(w, v)
            totals.append(total)
            accs.append(acc)
        for h, top, total, acc in zip(heads, tops, totals, accs):
            c = column(h)
            if h == PER + 1:
                out[j - first, :, c] = acc.astype(bf16)
                out[j - first, :, column(h + 1)] = stats_of(top, total, (BLOCK, DIM))
            else:
                out[j - first, :, c] = (acc / total).astype(bf16)


def by_block(info, pieces, queries, kv, q):
    here = info[1]
    return [(a, kv.at[here ^ d]) for d, a in enumerate(pieces)] + [(a, q.at[here ^ d]) for d, a in enumerate(queries)]


EARLY = [(j, h) for j in (2, 3) for h in range(MINE)]
LATE = [(j, h) for j in (0, 1) for h in range(MINE)]


def gather(info, p, q_in, f_in, kv, q, f, sems):
    pairs = by_block(info, p, q_in, kv, q) + [(a, f.at[d]) for d, a in enumerate(f_in)]
    fetch(pairs, sems)
    return [f.at[d] for d in range(XS)]


def early_kernel(info, fixed_ok, p0, p1, p2, p3, q0, q1, q2, q3, f0, f1, f2, f3, out, kv, q, f, sems):
    summary = gather(info, (p0, p1, p2, p3), (q0, q1, q2, q3), (f0, f1, f2, f3), kv, q, f, sems)
    attend(info, EARLY, kv, q, None, summary, fixed_ok, out, first=2)


def late_kernel(info, fixed_ok, halo, early, p0, p1, p2, p3, q0, q1, q2, q3, f0, f1, f2, f3, out, kv, q, f, sems):
    summary = gather(info, (p0, p1, p2, p3), (q0, q1, q2, q3), (f0, f1, f2, f3), kv, q, f, sems)
    attend(info, LATE, kv, q, halo, summary, fixed_ok, out)
    out[2:YS] = early[...]


def merge_kernel(back, far, out):
    for y in range(YS):
        for i, h in enumerate(heads_of(y)[:-1]):
            out[:, column(h)] = back[y, :, column(i)]
        near = back[y, :, column(MINE)].astype(f32)
        there = far[y, :, column(1)].astype(f32)
        near_top, near_total = near[:, 0:1], near[:, 1:2] + near[:, 2:3]
        far_top, far_total = there[:, 0:1], there[:, 1:2] + there[:, 2:3]
        top = jnp.maximum(near_top, far_top)
        near_scale, far_scale = jnp.exp2(near_top - top), jnp.exp2(far_top - top)
        acc = back[y, :, column(MINE - 1)].astype(f32) * near_scale
        acc = acc + far[y, :, column(0)].astype(f32) * far_scale
        total = near_total * near_scale + far_total * far_scale
        out[:, column(heads_of(y)[-1])] = (acc / total).astype(bf16)


VMEM = pl.BlockSpec(memory_space=pltpu.VMEM)
SMEM = pl.BlockSpec(memory_space=pltpu.SMEM)


ANY = pl.BlockSpec(memory_space=pl.ANY)


def call(kernel, shapes, flops, operands, scratch=(), left=0):
    many = isinstance(shapes, list)
    moved = sum(o.size * o.dtype.itemsize for o in operands)
    outs = [jax.ShapeDtypeStruct(s, bf16) for s in shapes] if many else jax.ShapeDtypeStruct(shapes, bf16)
    return pl.pallas_call(
        kernel,
        out_shape=outs,
        in_specs=[SMEM if o.ndim == 1 else VMEM for o in operands[: len(operands) - left]] + [ANY] * left,
        out_specs=[VMEM] * len(shapes) if many else VMEM,
        scratch_shapes=scratch,
        compiler_params=pltpu.CompilerParams(vmem_limit_bytes=(58 if left else 40) << 20),
        cost_estimate=pl.CostEstimate(flops=flops, bytes_accessed=moved, transcendentals=0),
        name=kernel.__name__,
    )(*operands)


tie = lax.optimization_barrier


def on_device(queries, key_states, value_states, key_keep, summary_pos):
    zp, zq, core, x, zh, y = (lax.axis_index(a) for a in AXES)
    window = (zp * ZQ + zq) * CORES + core
    group = window * (XS * ZH) + x * ZH + zh
    info = jnp.stack([(group > 0).astype(jnp.int32), y.astype(jnp.int32)])

    windows = jnp.arange(WINDOWS, dtype=jnp.int32)
    block_ids = group * YS + jnp.arange(YS, dtype=jnp.int32)
    fixed_ok = (windows * (XS * ZH * YS) + summary_pos)[None, :] < block_ids[:, None] - 2
    fixed_ok = jnp.repeat(fixed_ok.astype(f32), PART, axis=1)

    shapes = [(WINDOWS, PART, 3 * DIM), (XS * YS, PART, 2 * DIM)] + [(ROWS, WIDE)] * YS + [(BLOCK, WIDE)] * YS
    wide = pltpu.VMEM((BLOCK, HEADS * DIM), bf16)
    scratch = [wide, wide, wide, pltpu.SemaphoreType.DMA((3,))]
    rows = [info, key_keep.reshape(1, BLOCK), queries, key_states, value_states]
    packed = call(pack_kernel, shapes, 10**6, rows, scratch, left=3)
    s1, f1, pieces, asked = packed[0], packed[1], packed[2 : 2 + YS], packed[2 + YS :]
    root = jnp.sum(jnp.where(windows == window, summary_pos, 0))
    slot = jnp.arange(XS * YS, dtype=jnp.int32) == root // (ZH * YS) * YS + root % YS
    here = zh == root // YS % ZH

    got = [pieces[0]] + [send(pieces[d], flip("y", d)) for d in range(1, YS)]
    parts = lax.all_to_all(f1, ("x", "y"), 0, 0)
    parts, s1 = tie((parts, s1))
    part = lax.all_to_all(s1, GRP, 0, 0)
    piece = jnp.sum(jnp.where(slot[:, None, None], parts, 0).astype(f32), axis=0).astype(bf16)
    twin = send(piece, flip("zh", 1))
    spread = jnp.where(here, piece, twin)
    got1, got2, got3, part, spread = tie((got[1], got[2], got[3], part, spread))
    got = [got[0], got1, got2, got3]

    quarter = jnp.broadcast_to(part[None, :, :, : 2 * DIM], (YS, WINDOWS, PART, 2 * DIM))
    quarters = lax.all_to_all(quarter, ("zq", "core"), 0, 0)
    halo = call(halo_kernel, (2, 2 * BLOCK, WIDE), 10**6, [info] + got)
    halo = lax.ppermute(halo, AXES, leg(0))
    halo, quarters, spread = tie((halo, quarters, spread))
    halo = lax.ppermute(halo, AXES, leg(1))
    spread = jnp.broadcast_to(spread[None], (WINDOWS,) + spread.shape)
    spread = lax.all_to_all(spread, GRP, 0, 0).reshape(-1, 2 * DIM)
    part, halo = tie((part, halo))
    far = call(far_kernel, (WINDOWS, PART, 2 * DIM), 10**10, [part, quarters])
    halo, far, spread, asked = tie((halo, far, spread, asked))

    halo = lax.ppermute(halo, AXES, leg(2))
    asked = [asked[0]] + [send(asked[d], flip("y", d)) for d in range(1, YS)]
    scratch = [
        pltpu.VMEM((YS, ROWS, WIDE), bf16),
        pltpu.VMEM((YS, BLOCK, WIDE), bf16),
        pltpu.VMEM((XS, WINDOWS * PART, 2 * DIM), bf16),
        pltpu.SemaphoreType.DMA((2 * YS + XS,)),
    ]
    shape = (YS, BLOCK, WIDE + DIM)
    far = lax.all_to_all(far, GRP, 0, 0).reshape(YS, BLOCK, 2 * DIM)
    summary = [spread] + [send(spread, flip("x", d)) for d in range(1, XS)]
    rest = got + asked + summary
    early = call(early_kernel, (2,) + shape[1:], 3 * 10**8, [info, fixed_ok] + rest, scratch, left=len(rest))
    halo, early = tie((halo, early))
    out = call(late_kernel, shape, 10**10, [info, fixed_ok, halo, early] + rest, scratch, left=len(rest))
    out, far = tie((out, far))
    back = lax.all_to_all(out, "y", 0, 0)
    return call(merge_kernel, queries.shape, 10**6, [back, far])


def solution(mesh):
    fine = Mesh(mesh.devices.reshape(tuple(SIZES.values())), AXES)
    return jax.shard_map(
        on_device,
        mesh=fine,
        in_specs=(P(AXES, None), P(AXES, None), P(AXES, None), P(AXES), P()),
        out_specs=P(AXES, None),
        check_vma=False,
    )
```
